256 devices in a mesh: re: 8 (over x, y_lo), rp: 16 (over z, core), mode: 2 (over y_hi).
Axes of the slice: x: 4, y: 4 (y_hi: 2, y_lo: 2; y = y_hi * 2 + y_lo), z: 8, core: 2. Of those that a mesh axis runs over, the one named last changes fastest.
Arguments:
- coupling: float32 [2, 64, 16, 120, 576], P(None, 're', 'rp', 'mode'), may hold values from -0.1875 to 0.1875
- electron_cells: int32 [64, 3], replicated, may hold values from -6 to 6
- phonon_cells: int32 [16, 3], replicated, may hold values from -3 to 3
- kpoint_index: int32 [16, 3], replicated, may hold values from 0 to 15
- qpoint_index: int32 [16, 3], replicated, may hold values from 0 to 15
- eigenvectors: float32 [16, 2, 120, 120], P('rp', None, 'mode'), may hold values from -0.5 to 0.5
- frequencies: float32 [16, 120], P('rp', 'mode'), may hold values from 0.25 to 2
Outputs:
- mode_coupling: float32 [120, 16, 16, 2, 576], P('mode', 'rp', 're')
The draws below stay inside these ranges and needn't reach their ends.
All inputs are finite; a program needn't handle non-finite values.
Results may differ from the reference program's by a relative error of at most 0.00007.
Values sent between devices are 32-bit elements; how exact they have to be, the bound alone decides.
No kernel may reach another device: no remote copies, remote signals or barrier semaphores. Data moves between devices by JAX's collectives and lax.ppermute only.
A program may use at most 64 MiB of HBM per device.

```python
import math
import jax
import jax.numpy as jnp
from jax import lax

P_SIZE = 576
MODES = 120
KG = 16
NRE = 64
NRP = 16
NK = 16
NQ = 16


def touch_ends(result, key, smallest, high):
    longest = result.shape.index(max(result.shape))
    spots = []
    for shift in (0, 1):
        where = [jax.random.randint(jax.random.fold_in(key, axis), (), 0, length) for axis, length in enumerate(result.shape)]
        where[longest] = (where[longest] + shift) % result.shape[longest]
        spots.append(tuple(where))
    return result.at[spots[0]].set(smallest).at[spots[1]].set(high)


def steps_of(rng, extent, cuts, low, high):
    gain = 1.0
    for axis_at, parts in cuts:
        heights = jax.random.uniform(jax.random.fold_in(jax.random.fold_in(rng, 6), axis_at), (parts,), jnp.float32, low / len(cuts), high / len(cuts))
        gain = gain * jnp.repeat(jnp.exp(heights), extent[axis_at] // parts).reshape((-1,) + (1,) * (len(extent) - 1 - axis_at))
    return gain


def gaussian(rng, shape, scale, reach, shards=(), dtype=jnp.bfloat16):
    level = steps_of(rng, shape, shards, -0.22, 0.18) if shards else 1.0
    values = jax.random.normal(rng, shape, jnp.float32) * scale * level
    return jnp.minimum(jnp.maximum(values, -reach), reach).astype(dtype)


def setup_inputs(seed: int = 0) -> dict:
    keys = jax.random.split(jax.random.key(seed), 8)
    return {
        "coupling": gaussian(keys[0], (2, NRE, NRP, MODES, P_SIZE), (NRE * NRP) ** -0.5, 0.1875, ((1, 8), (2, 16), (3, 2)), jnp.float32),
        "electron_cells": touch_ends(jax.random.randint(keys[1], (NRE, 3), -6, 7), jax.random.fold_in(keys[1], 1), -6, 6).astype(jnp.int32),
        "phonon_cells": touch_ends(jax.random.randint(keys[2], (NRP, 3), -3, 4), jax.random.fold_in(keys[2], 1), -3, 3).astype(jnp.int32),
        "kpoint_index": touch_ends(jax.random.randint(keys[3], (NK, 3), 0, KG), jax.random.fold_in(keys[3], 1), 0, KG - 1).astype(jnp.int32),
        "qpoint_index": touch_ends(jax.random.randint(keys[4], (NQ, 3), 0, KG), jax.random.fold_in(keys[4], 1), 0, KG - 1).astype(jnp.int32),
        "eigenvectors": gaussian(keys[5], (NQ, 2, MODES, MODES), MODES ** -0.5, 0.5, ((0, 16), (2, 2)), jnp.float32),
        "frequencies": jnp.clip(jnp.exp(math.log(2.0) - 2.0794415 * jax.random.uniform(keys[6], (NQ, MODES), jnp.float32) ** steps_of(keys[6], (NQ, MODES), ((0, 16), (1, 2)), -0.2, 0.2)), 0.25, 2.0),
    }


def phases(points, cells):
    turns = lax.optimization_barrier(jnp.sum(points[:, None, :] * cells[None, :, :], axis=-1)) % KG
    angle = turns.astype(jnp.float32) * (2.0 * 3.141592653589793 / KG)
    return (jnp.cos(angle), jnp.sin(angle))

def reference(coupling, electron_cells, phonon_cells, kpoint_index, qpoint_index, eigenvectors, frequencies):
    hp = lax.Precision.HIGHEST
    cos_e, sin_e = phases(kpoint_index, electron_cells)
    real_part = coupling[0].reshape(NRE, -1)
    imag_part = coupling[1].reshape(NRE, -1)
    bk_real = jnp.dot(cos_e, real_part, precision=hp) - jnp.dot(sin_e, imag_part, precision=hp)
    bk_imag = jnp.dot(cos_e, imag_part, precision=hp) + jnp.dot(sin_e, real_part, precision=hp)
    bk_real = bk_real.reshape(NK, NRP, MODES, P_SIZE)
    bk_imag = bk_imag.reshape(NK, NRP, MODES, P_SIZE)
    cos_p, sin_p = phases(qpoint_index, phonon_cells)
    kq_real = jnp.einsum('qs,kscp->qkcp', cos_p, bk_real, precision=hp) - jnp.einsum('qs,kscp->qkcp', sin_p, bk_imag, precision=hp)
    kq_imag = jnp.einsum('qs,kscp->qkcp', cos_p, bk_imag, precision=hp) + jnp.einsum('qs,kscp->qkcp', sin_p, bk_real, precision=hp)
    vec_real = eigenvectors[:, 0]
    vec_imag = eigenvectors[:, 1]
    out_real = jnp.einsum('qkcp,qcn->nqkp', kq_real, vec_real, precision=hp) - jnp.einsum('qkcp,qcn->nqkp', kq_imag, vec_imag, precision=hp)
    out_imag = jnp.einsum('qkcp,qcn->nqkp', kq_real, vec_imag, precision=hp) + jnp.einsum('qkcp,qcn->nqkp', kq_imag, vec_real, precision=hp)
    factor = lax.rsqrt(2.0 * frequencies).T[:, :, None, None]
    return jnp.stack([out_real * factor, out_imag * factor], axis=3)
```

```python
import jax
import jax.numpy as jnp
from jax import lax
from jax.sharding import PartitionSpec as P

KG = 16
HP = lax.Precision.HIGHEST
LANES = 128


def phases(points, cells):
    turns = jnp.sum(points[:, None, :] * cells[None, :, :], axis=-1) % KG
    angle = turns.astype(jnp.float32) * (2.0 * 3.141592653589793 / KG)
    return (jnp.cos(angle), jnp.sin(angle))


def rotation(points, cells):
    cos_t, sin_t = phases(points, cells)
    upper = jnp.stack([cos_t, -sin_t], axis=-1)
    lower = jnp.stack([sin_t, cos_t], axis=-1)
    return jnp.stack([upper, lower], axis=1)


def exchange(parts, axis):
    return lax.all_to_all(parts, axis, split_axis=0, concat_axis=0, tiled=True)


def shards(
    coupling, electron_cells, phonon_cells, kpoint_index, qpoint_index, eigenvectors, frequencies
):
    re_size = lax.axis_size("re")
    rp_size = lax.axis_size("rp")
    _, re_local, _, modes_local, pairs = coupling.shape
    nk = kpoint_index.shape[0]
    nq = qpoint_index.shape[0]
    nre = electron_cells.shape[0]
    nrp = phonon_cells.shape[0]
    columns = modes_local * pairs
    piece = -(-columns // (re_size * LANES))
    padded = piece * re_size * LANES

    scale = lax.rsqrt(2.0 * frequencies[0])
    mine = lax.axis_index("mode")
    other_vec = lax.ppermute(eigenvectors[0], "mode", [(0, 1), (1, 0)])
    other_scale = lax.ppermute(scale, "mode", [(0, 1), (1, 0)])
    pair_vec = jnp.stack([eigenvectors[0], other_vec])
    vec = jnp.where(mine == 0, pair_vec, pair_vec[::-1])
    vec = jnp.moveaxis(vec, 0, 1).reshape(2, 2 * modes_local, -1)
    pair_scale = jnp.stack([scale, other_scale])
    scales = jnp.where(mine == 0, pair_scale, pair_scale[::-1]).reshape(-1)
    vec = vec * scales[None, None, :]

    flat = coupling.reshape(2, re_local, columns)
    flat = jnp.pad(flat, ((0, 0), (0, 0), (0, padded - columns)))
    flat = flat.reshape(2, re_local, re_size, piece, LANES).transpose(2, 1, 0, 3, 4)
    got = exchange(flat, "re")
    rot_e = rotation(kpoint_index, electron_cells).reshape(nk * 2, nre * 2)
    bloch_k = jnp.einsum(
        "kr,rab->kab", rot_e, got.reshape(nre * 2, piece, LANES), precision=HP
    )

    got = exchange(bloch_k.reshape(nk, 2, piece, LANES), "rp")
    rot_p = rotation(qpoint_index, phonon_cells).reshape(nq * 2, nrp * 2)
    bloch_kq = jnp.einsum(
        "qs,sab->qab", rot_p, got.reshape(nrp * 2, piece, LANES), precision=HP
    )

    got = exchange(bloch_kq.reshape(nq, 2, piece, LANES), "rp")
    got = exchange(got, ("re", "mode"))
    got = got.reshape(re_size, 2, 2, piece, LANES).transpose(2, 1, 0, 3, 4)
    got = got.reshape(2, 2, padded)[:, :, :columns].reshape(2, 2 * modes_local, pairs)

    real = jnp.stack([vec[0], -vec[1]])
    imag = jnp.stack([vec[1], vec[0]])
    matrix = jnp.stack([real, imag])

    def rotate(start):
        half = lax.dynamic_slice_in_dim(matrix, start * modes_local, modes_local, 3)
        return jnp.einsum("gbcn,bcp->ngp", half, got, precision=HP)

    theirs = lax.ppermute(rotate(1 - mine), "mode", [(0, 1), (1, 0)])
    ours = rotate(mine)
    both = jnp.stack([ours, theirs], axis=1)
    both = jnp.where(mine == 0, both, both[:, ::-1])
    return both[:, None]


def solution(mesh):
    placed = (
        P(None, "re", "rp", "mode", None),
        P(),
        P(),
        P(),
        P(),
        P("rp", None, "mode", None),
        P("rp", "mode"),
    )
    return jax.shard_map(
        shards,
        mesh=mesh,
        in_specs=placed,
        out_specs=P("mode", "rp", "re", None, None),
        check_vma=False,
    )
```

```python
import functools

import jax
import jax.numpy as jnp
from jax import lax
from jax.experimental import pallas as pl
from jax.experimental.pallas import tpu as pltpu
from jax.sharding import PartitionSpec as P

KG = 16
HP = lax.Precision.HIGHEST
LANES = 128
HALF = 64


def phases(points, cells):
    turns = jnp.sum(points[:, None, :] * cells[None, :, :], axis=-1) % KG
    angle = turns.astype(jnp.float32) * (2.0 * 3.141592653589793 / KG)
    return jnp.concatenate([jnp.cos(angle), jnp.sin(angle)], axis=0)


def exchange(parts, axis):
    return lax.all_to_all(parts, axis, split_axis=0, concat_axis=0, tiled=True)


def turn(table, block, count):
    both = jnp.dot(table, block, precision=HP, preferred_element_type=jnp.float32)
    parts = []
    for at in range(0, block.shape[1], LANES):
        cos_part = both[:count, at : at + LANES]
        sin_part = pltpu.roll(both[count:, at : at + LANES], HALF, 1)
        lane = lax.broadcasted_iota(jnp.int32, sin_part.shape, 1)
        parts.append(cos_part + jnp.where(lane < HALF, -sin_part, sin_part))
    return parts


def lay_out(x_ref, o_ref, held):
    r = pl.program_id(0)
    count = pl.num_programs(0)
    modes, pairs = x_ref.shape[-2:]

    @pl.when(r == 0)
    def _():
        held[...] = jnp.zeros_like(held)

    held[:modes] = x_ref[0, 0, 0]
    held[HALF : HALF + modes] = x_ref[1, 0, 0]
    o_ref[pl.ds(r, pairs, stride=8), :] = held[...].T


def electron(g_ref, x_ref, o_ref, *, nk, src, span):
    step = pl.program_id(0)
    for m in range(2):
        cols = []
        for p in range(span):
            rows = [x_ref[i * 2 + m, p] for i in range(src)]
            cols.append(jnp.concatenate(rows, axis=0))
        parts = turn(g_ref[...], jnp.concatenate(cols, axis=1), nk)
        total = o_ref.shape[0] // nk
        for p in range(span):
            at = (step * span + p) * 2 + m
            o_ref[pl.ds(at, nk, stride=total), :] = parts[p]


def phonon(g_ref, x_ref, o_ref, *, nq, ns):
    rows = x_ref.shape[0] // ns
    group = 8
    for start in range(0, rows, group):
        cols = [x_ref[pl.ds(start + t, ns, stride=rows), :] for t in range(group)]
        parts = turn(g_ref[...], jnp.concatenate(cols, axis=1), nq)
        for t in range(group):
            o_ref[pl.ds(start + t, nq, stride=rows), :] = parts[t]


def modes_of(x_ref, w_ref, o_ref, *, nk, pts, kk):
    count = nk * pts
    x = jnp.concatenate(
        [x_ref[pl.ds(0, count, stride=2), :], x_ref[pl.ds(1, count, stride=2), :]], axis=1
    )
    res = jnp.dot(x, w_ref[...], precision=HP, preferred_element_type=jnp.float32)
    for k in range(nk):
        for m in range(2):
            base = ((k // kk) * 2 + m) * pts * kk + k % kk
            o_ref[pl.ds(base, pts, stride=kk), :] = res[
                k * pts : (k + 1) * pts, m * LANES : (m + 1) * LANES
            ]


def finish(x_ref, o_ref, *, kk):
    modes, _, _, _, pairs = o_ref.shape
    for k in range(kk):
        turned = x_ref[pl.ds(k, pairs, stride=kk), :].T
        o_ref[:, 0, k, 0, :] = turned[:modes]
        o_ref[:, 0, k, 1, :] = turned[HALF : HALF + modes]


def call(body, out_shape, *args, **kw):
    return pl.pallas_call(
        body, out_shape=jax.ShapeDtypeStruct(out_shape, jnp.float32), **kw
    )(*args)


def shards(
    coupling, electron_cells, phonon_cells, kpoint_index, qpoint_index, eigenvectors, frequencies
):
    re_size = lax.axis_size("re")
    rp_size = lax.axis_size("rp")
    _, nr, _, modes, pairs = coupling.shape
    nk = kpoint_index.shape[0]
    nq = qpoint_index.shape[0]
    ns = phonon_cells.shape[0]
    peers = re_size * 2
    pts = pairs // peers
    kk = nk // re_size

    packed = jnp.concatenate(
        [eigenvectors[0].reshape(2 * modes, -1), jnp.pad(frequencies, ((0, 0), (0, modes)))]
    )
    other = lax.ppermute(packed, "mode", [(0, 1), (1, 0)])
    both = jnp.stack([packed, other])
    both = jnp.where(lax.axis_index("mode") == 0, both, both[::-1])
    scale = lax.rsqrt(2.0 * both[:, -1, :modes]).reshape(-1)
    vec = both[:, :-1].reshape(2, 2, modes, 2 * modes) * scale
    real = jnp.stack([vec[:, 0], -vec[:, 1]], axis=1)
    imag = jnp.stack([vec[:, 1], vec[:, 0]], axis=1)
    weight = jnp.stack([real, imag], axis=3)
    weight = weight.reshape(2, 2, modes, 2, 2, modes).transpose(0, 1, 2, 4, 3, 5)
    gap = HALF - modes
    weight = jnp.pad(weight, ((0, 0), (0, 0), (0, gap), (0, 0), (0, 0), (0, gap)))
    weight = weight.reshape(2 * LANES, 2 * LANES)

    laid = call(
        lay_out,
        (pairs * nr, LANES),
        coupling,
        grid=(nr,),
        in_specs=[pl.BlockSpec((2, 1, 1, modes, pairs), lambda r: (0, r, 0, 0, 0))],
        out_specs=pl.BlockSpec((pairs * nr, LANES), lambda r: (0, 0)),
        scratch_shapes=[pltpu.VMEM((LANES, pairs), jnp.float32)],
    )
    got = exchange(laid.reshape(peers, pts * nr, LANES), ("re", "mode"))
    span = 9
    bloch_k = call(
        functools.partial(electron, nk=nk, src=re_size, span=span),
        (nk * pts * 2, LANES),
        phases(kpoint_index, electron_cells),
        got.reshape(peers, pts, nr, LANES),
        grid=(pts // span,),
        in_specs=[
            pl.BlockSpec((2 * nk, re_size * nr), lambda i: (0, 0)),
            pl.BlockSpec((peers, span, nr, LANES), lambda i: (0, i, 0, 0)),
        ],
        out_specs=pl.BlockSpec((nk * pts * 2, LANES), lambda i: (0, 0)),
    )

    got = exchange(bloch_k.reshape(rp_size, pts * 2, LANES), "rp")
    bloch_kq = call(
        functools.partial(phonon, nq=nq, ns=ns),
        (nq * pts * 2, LANES),
        phases(qpoint_index, phonon_cells),
        got.reshape(ns * pts * 2, LANES),
    )

    got = exchange(bloch_kq.reshape(rp_size, pts * 2, LANES), "rp")
    rotated = call(
        functools.partial(modes_of, nk=nk, pts=pts, kk=kk),
        (peers * pts * kk, LANES),
        got.reshape(nk * pts * 2, LANES),
        weight,
    )

    got = exchange(rotated.reshape(peers, pts * kk, LANES), ("re", "mode"))
    return call(
        functools.partial(finish, kk=kk),
        (modes, 1, kk, 2, pairs),
        got.reshape(pairs * kk, LANES),
    )


def solution(mesh):
    placed = (
        P(None, "re", "rp", "mode", None),
        P(),
        P(),
        P(),
        P(),
        P("rp", None, "mode", None),
        P("rp", "mode"),
    )
    return jax.shard_map(
        shards,
        mesh=mesh,
        in_specs=placed,
        out_specs=P("mode", "rp", "re", None, None),
        check_vma=False,
    )
```

```python
import functools

import jax
import jax.numpy as jnp
from jax import lax
from jax.experimental import pallas as pl
from jax.experimental.pallas import tpu as pltpu
from jax.sharding import PartitionSpec as P

KG = 16
HP = lax.Precision.HIGHEST
LANES = 128
HALF = 64


def phases(points, cells):
    turns = jnp.sum(points[:, None, :] * cells[None, :, :], axis=-1) % KG
    angle = turns.astype(jnp.float32) * (2.0 * 3.141592653589793 / KG)
    return jnp.concatenate([jnp.cos(angle), jnp.sin(angle)], axis=0)


def exchange(parts, axis):
    return lax.all_to_all(parts, axis, split_axis=0, concat_axis=0, tiled=True)


def turn(table, block, count):
    both = jnp.dot(table, block, precision=HP, preferred_element_type=jnp.float32)
    parts = []
    for at in range(0, block.shape[1], LANES):
        cos_part = both[:count, at : at + LANES]
        sin_part = pltpu.roll(both[count:, at : at + LANES], HALF, 1)
        lane = lax.broadcasted_iota(jnp.int32, sin_part.shape, 1)
        parts.append(cos_part + jnp.where(lane < HALF, -sin_part, sin_part))
    return parts


def lay_out(x_ref, o_ref, held):
    r = pl.program_id(0)
    count = pl.num_programs(0)
    modes, _, pairs = x_ref.shape[-3:]

    @pl.when(r == 0)
    def _():
        held[...] = jnp.zeros_like(held)

    held[:modes] = x_ref[0, 0, :, 0, :]
    held[HALF : HALF + modes] = x_ref[1, 0, :, 0, :]
    o_ref[pl.ds(r, pairs, stride=8), :] = held[...].T


def electron(g_ref, x_ref, o_ref, *, nk, src):
    points = o_ref.shape[0] // nk
    group = 8
    for start in range(0, points, group):
        cols = []
        for p in range(start, start + group):
            cols.append(jnp.concatenate([x_ref[i, p] for i in range(src)], axis=0))
        parts = turn(g_ref[...], jnp.concatenate(cols, axis=1), nk)
        for t in range(group):
            o_ref[pl.ds(start + t, nk, stride=points), :] = parts[t]


def phonon(g_ref, x_ref, o_ref, *, nq, ns):
    rows = x_ref.shape[0] // ns
    group = 8
    for start in range(0, rows, group):
        cols = [x_ref[pl.ds(start + t, ns, stride=rows), :] for t in range(group)]
        parts = turn(g_ref[...], jnp.concatenate(cols, axis=1), nq)
        for t in range(group):
            o_ref[pl.ds(start + t, nq, stride=rows), :] = parts[t]


def modes_of(x_ref, w_ref, o_ref, *, nk, pts, kk):
    for k in range(nk):
        at = 2 * k * pts
        x = jnp.concatenate(
            [x_ref[at : at + pts, :], x_ref[at + pts : at + 2 * pts, :]], axis=1
        )
        res = jnp.dot(x, w_ref[...], precision=HP, preferred_element_type=jnp.float32)
        for m in range(2):
            base = ((k // kk) * 2 + m) * pts * kk + k % kk
            o_ref[pl.ds(base, pts, stride=kk), :] = res[:, m * LANES : (m + 1) * LANES]


def finish(x_ref, o_ref, *, kk):
    modes, _, _, _, pairs = o_ref.shape
    for k in range(kk):
        turned = x_ref[pl.ds(k, pairs, stride=kk), :].T
        o_ref[:, 0, k, 0, :] = turned[:modes]
        o_ref[:, 0, k, 1, :] = turned[HALF : HALF + modes]


WHOLE = pl.BlockSpec(memory_space=pltpu.VMEM)


def near(x):
    return pltpu.with_memory_space_constraint(x, pltpu.VMEM)


def call(body, out_shape, *args, **kw):
    return pl.pallas_call(body, out_shape=pltpu.VMEM(out_shape, jnp.float32), **kw)(*args)


def shards(
    coupling, electron_cells, phonon_cells, kpoint_index, qpoint_index, eigenvectors, frequencies
):
    re_size = lax.axis_size("re")
    rp_size = lax.axis_size("rp")
    _, nr, _, modes, pairs = coupling.shape
    nk = kpoint_index.shape[0]
    nq = qpoint_index.shape[0]
    ns = phonon_cells.shape[0]
    peers = re_size * 2
    pts = pairs // peers
    kk = nk // re_size

    packed = jnp.concatenate(
        [eigenvectors[0].reshape(2 * modes, -1), jnp.pad(frequencies, ((0, 0), (0, modes)))]
    )
    other = lax.ppermute(packed, "mode", [(0, 1), (1, 0)])
    both = jnp.stack([packed, other])
    both = jnp.where(lax.axis_index("mode") == 0, both, both[::-1])
    scale = lax.rsqrt(2.0 * both[:, -1, :modes]).reshape(-1)
    vec = both[:, :-1].reshape(2, 2, modes, 2 * modes) * scale
    real = jnp.stack([vec[:, 0], -vec[:, 1]], axis=1)
    imag = jnp.stack([vec[:, 1], vec[:, 0]], axis=1)
    weight = jnp.stack([real, imag], axis=3)
    weight = weight.reshape(2, 2, modes, 2, 2, modes).transpose(0, 1, 2, 4, 3, 5)
    gap = HALF - modes
    weight = jnp.pad(weight, ((0, 0), (0, 0), (0, gap), (0, 0), (0, 0), (0, gap)))
    weight = weight.reshape(2 * LANES, 2 * LANES)

    laid = call(
        lay_out,
        (pairs * nr, LANES),
        coupling.transpose(0, 1, 3, 2, 4),
        grid=(nr,),
        in_specs=[pl.BlockSpec((2, 1, modes, 1, pairs), lambda r: (0, r, 0, 0, 0))],
        out_specs=pl.BlockSpec((pairs * nr, LANES), lambda r: (0, 0)),
        scratch_shapes=[pltpu.VMEM((LANES, pairs), jnp.float32)],
    )
    got = exchange(laid.reshape(re_size, 2 * pts * nr, LANES), "re")
    bloch_k = call(
        functools.partial(electron, nk=nk, src=re_size),
        (nk * pts * 2, LANES),
        phases(kpoint_index, electron_cells),
        near(got.reshape(re_size, 2 * pts, nr, LANES)),
        in_specs=[WHOLE, WHOLE],
        out_specs=WHOLE,
    )

    got = exchange(bloch_k.reshape(rp_size, pts * 2, LANES), "rp")
    bloch_kq = call(
        functools.partial(phonon, nq=nq, ns=ns),
        (nq * pts * 2, LANES),
        phases(qpoint_index, phonon_cells),
        near(got.reshape(ns * pts * 2, LANES)),
        in_specs=[WHOLE, WHOLE],
        out_specs=WHOLE,
    )

    got = exchange(bloch_kq.reshape(rp_size * 2, pts // 4, 4, LANES), ("rp", "mode"))
    rotated = call(
        functools.partial(modes_of, nk=nk, pts=pts, kk=kk),
        (peers * pts * kk, LANES),
        near(got.reshape(nk * pts * 2, LANES)),
        weight,
        in_specs=[WHOLE, WHOLE],
        out_specs=WHOLE,
    )

    got = exchange(rotated.reshape(peers, pts * kk, LANES), ("re", "mode"))
    return pl.pallas_call(
        functools.partial(finish, kk=kk),
        out_shape=jax.ShapeDtypeStruct((modes, 1, kk, 2, pairs), jnp.float32),
        in_specs=[WHOLE],
        out_specs=WHOLE,
    )(near(got.reshape(pairs * kk, LANES)))


def solution(mesh):
    placed = (
        P(None, "re", "rp", "mode", None),
        P(),
        P(),
        P(),
        P(),
        P("rp", None, "mode", None),
        P("rp", "mode"),
    )
    return jax.shard_map(
        shards,
        mesh=mesh,
        in_specs=placed,
        out_specs=P("mode", "rp", "re", None, None),
        check_vma=False,
    )
```

```python
import functools

import jax
import jax.numpy as jnp
from jax import lax
from jax.experimental import pallas as pl
from jax.experimental.pallas import tpu as pltpu
from jax.sharding import PartitionSpec as P

KG = 16
LANES = 128
HALF = 64


def exchange(parts, axis):
    return lax.all_to_all(parts, axis, split_axis=0, concat_axis=0, tiled=True)


def split(x):
    high = x.astype(jnp.bfloat16)
    return high, (x - high.astype(jnp.float32)).astype(jnp.bfloat16)


def dot(a, b):
    return jnp.dot(a, b, preferred_element_type=jnp.float32)


def phases(points_ref, cells_ref, stride=1):
    points = points_ref[...].astype(jnp.float32)
    count = points.shape[1]
    if stride > 1:
        old = lax.broadcasted_iota(jnp.int32, (count, count), 0)
        new = lax.broadcasted_iota(jnp.int32, (count, count), 1)
        at = old % stride * (count // stride) + old // stride
        points = jnp.dot(
            points, jnp.where(at == new, 1.0, 0.0), precision=lax.Precision.HIGHEST
        )
    exact = lax.dot_general(
        points,
        cells_ref[...].astype(jnp.float32),
        (((0,), (0,)), ((), ())),
        precision=lax.Precision.HIGHEST,
        preferred_element_type=jnp.float32,
    )
    turns = exact.astype(jnp.int32) & (KG - 1)
    angle = turns.astype(jnp.float32) * (2.0 * 3.141592653589793 / KG)
    high, low = split(jnp.concatenate([jnp.cos(angle), jnp.sin(angle)], axis=0))
    return jnp.concatenate([high, high, low], axis=1)


def turn(table, block, count):
    high, low = split(block)
    both = dot(table, jnp.concatenate([high, low, high], axis=0))
    parts = []
    for at in range(0, block.shape[1], LANES):
        cos_part = both[:count, at : at + LANES]
        sin_part = pltpu.roll(both[count:, at : at + LANES], HALF, 1)
        lane = lax.broadcasted_iota(jnp.int32, sin_part.shape, 1)
        parts.append(cos_part + jnp.where(lane < HALF, -sin_part, sin_part))
    return parts


def lay_out(x_ref, o_ref, buf, held, sems):
    _, nr, modes, _, pairs = x_ref.shape
    copies = [
        pltpu.make_async_copy(x_ref.at[:, r], buf.at[r], sems.at[r]) for r in range(nr)
    ]
    for copy in copies:
        copy.start()
    held[...] = jnp.zeros_like(held)
    for r in range(nr):
        copies[r].wait()
        slot = r % 2
        held[slot, :modes] = buf[r, 0, :, 0, :]
        held[slot, HALF : HALF + modes] = buf[r, 1, :, 0, :]
        o_ref[pl.ds(r, pairs, stride=nr), :] = held[slot].T


def electron(k_ref, c_ref, x_ref, o_ref, *, kk):
    src, points = x_ref.shape[:2]
    nk = k_ref.shape[1]
    table = phases(k_ref, c_ref, kk)
    group = 8
    for start in range(0, points, group):
        cols = []
        for p in range(start, start + group):
            cols.append(jnp.concatenate([x_ref[i, p] for i in range(src)], axis=0))
        parts = turn(table, jnp.concatenate(cols, axis=1), nk)
        for t in range(group):
            o_ref[pl.ds(start + t, nk, stride=points), :] = parts[t]


def phonon(q_ref, c_ref, x_ref, o_ref):
    nq, ns = q_ref.shape[1], c_ref.shape[1]
    rows = x_ref.shape[0] // ns
    table = phases(q_ref, c_ref)
    group = 8
    for start in range(0, rows, group):
        cols = [x_ref[pl.ds(start + t, ns, stride=rows), :] for t in range(group)]
        parts = turn(table, jnp.concatenate(cols, axis=1), nq)
        for t in range(group):
            o_ref[pl.ds(start + t, nq, stride=rows), :] = parts[t]


def modes_of(x_ref, w_ref, o_ref, *, nk, pts, kk):
    owners = nk // kk
    w_high, w_low = split(w_ref[...])
    group = 9
    for start in range(0, pts, group):
        rows = []
        for p in range(start, start + group):
            both = [x_ref[pl.ds(m * pts + p, nk, stride=2 * pts), :] for m in range(2)]
            rows.append(jnp.concatenate(both, axis=1))
        high, low = split(jnp.concatenate(rows, axis=0))
        res = dot(high, w_high) + (dot(high, w_low) + dot(low, w_high))
        for t in range(group):
            for k in range(kk):
                at = t * nk + k * owners
                for m in range(2):
                    base = m * pts * kk + (start + t) * kk + k
                    o_ref[pl.ds(base, owners, stride=2 * pts * kk), :] = res[
                        at : at + owners, m * LANES : (m + 1) * LANES
                    ]


def finish(x_ref, o_ref, *, kk):
    modes, _, _, _, pairs = o_ref.shape
    for k in range(kk):
        turned = x_ref[pl.ds(k, pairs, stride=kk), :].T
        o_ref[:, 0, k, 0, :] = turned[:modes]
        o_ref[:, 0, k, 1, :] = turned[HALF : HALF + modes]


WHOLE = pl.BlockSpec(memory_space=pltpu.VMEM)
ROOM = pltpu.CompilerParams(vmem_limit_bytes=20 * 2**20)


def near(x):
    return pltpu.with_memory_space_constraint(x, pltpu.VMEM)


def call(body, rows, *args):
    return pl.pallas_call(
        body,
        out_shape=pltpu.VMEM((rows, LANES), jnp.float32),
        in_specs=[WHOLE] * len(args),
        out_specs=WHOLE,
        compiler_params=ROOM,
    )(*args)


def shards(
    coupling, electron_cells, phonon_cells, kpoint_index, qpoint_index, eigenvectors, frequencies
):
    re_size = lax.axis_size("re")
    rp_size = lax.axis_size("rp")
    _, nr, _, modes, pairs = coupling.shape
    nk = kpoint_index.shape[0]
    nq = qpoint_index.shape[0]
    ns = phonon_cells.shape[0]
    peers = re_size * 2
    pts = pairs // peers
    kk = nk // re_size

    laid = pl.pallas_call(
        lay_out,
        out_shape=pltpu.VMEM((pairs * nr, LANES), jnp.float32),
        in_specs=[pl.BlockSpec(memory_space=pltpu.HBM)],
        out_specs=WHOLE,
        compiler_params=ROOM,
        scratch_shapes=[
            pltpu.VMEM((nr, 2, modes, 1, pairs), jnp.float32),
            pltpu.VMEM((2, LANES, pairs), jnp.float32),
            pltpu.SemaphoreType.DMA((nr,)),
        ],
    )(coupling.transpose(0, 1, 3, 2, 4))
    got = exchange(laid.reshape(re_size, 2 * pts * nr, LANES), "re")
    small = (electron_cells, phonon_cells, kpoint_index, qpoint_index, eigenvectors, frequencies)
    got, small = lax.optimization_barrier((got, small))
    electron_cells, phonon_cells, kpoint_index, qpoint_index, eigenvectors, frequencies = small
    bloch_k = call(
        functools.partial(electron, kk=kk),
        nk * pts * 2,
        kpoint_index.T,
        electron_cells.T,
        near(got.reshape(re_size, 2 * pts, nr, LANES)),
    )

    packed = jnp.concatenate(
        [eigenvectors[0].reshape(2 * modes, -1), jnp.pad(frequencies, ((0, 0), (0, modes)))]
    )
    other = lax.ppermute(packed, "mode", [(0, 1), (1, 0)])
    both = jnp.stack([packed, other])
    both = jnp.where(lax.axis_index("mode") == 0, both, both[::-1])
    scale = lax.rsqrt(2.0 * both[:, -1, :modes]).reshape(-1)
    vec = both[:, :-1].reshape(2, 2, modes, 2 * modes) * scale
    real = jnp.stack([vec[:, 0], -vec[:, 1]], axis=1)
    imag = jnp.stack([vec[:, 1], vec[:, 0]], axis=1)
    weight = jnp.stack([real, imag], axis=3)
    weight = weight.reshape(2, 2, modes, 2, 2, modes).transpose(0, 1, 2, 4, 3, 5)
    gap = HALF - modes
    weight = jnp.pad(weight, ((0, 0), (0, 0), (0, gap), (0, 0), (0, 0), (0, gap)))
    weight = weight.reshape(2 * LANES, 2 * LANES)

    got = exchange(bloch_k.reshape(rp_size, pts * 2, LANES), "rp")
    bloch_kq = call(
        phonon,
        nq * pts * 2,
        qpoint_index.T,
        phonon_cells.T,
        near(got.reshape(ns * pts * 2, LANES)),
    )

    got = exchange(bloch_kq.reshape(rp_size * 2, pts // 4, 4, LANES), ("rp", "mode"))
    rotated = call(
        functools.partial(modes_of, nk=nk, pts=pts, kk=kk),
        peers * pts * kk,
        near(got.reshape(nk * pts * 2, LANES)),
        weight,
    )

    got = exchange(rotated.reshape(peers, pts * kk, LANES), ("re", "mode"))
    return pl.pallas_call(
        functools.partial(finish, kk=kk),
        out_shape=jax.ShapeDtypeStruct((modes, 1, kk, 2, pairs), jnp.float32),
        in_specs=[WHOLE],
        out_specs=WHOLE,
        compiler_params=ROOM,
    )(near(got.reshape(pairs * kk, LANES)))


def solution(mesh):
    placed = (
        P(None, "re", "rp", "mode", None),
        P(),
        P(),
        P(),
        P(),
        P("rp", None, "mode", None),
        P("rp", "mode"),
    )
    return jax.shard_map(
        shards,
        mesh=mesh,
        in_specs=placed,
        out_specs=P("mode", "rp", "re", None, None),
        check_vma=False,
    )
```

```python
import functools

import jax
import jax.numpy as jnp
from jax import lax
from jax.experimental import pallas as pl
from jax.experimental.pallas import tpu as pltpu
from jax.sharding import PartitionSpec as P

KG = 16
LANES = 128
HALF = 64


def exchange(parts, axis):
    return lax.all_to_all(parts, axis, split_axis=0, concat_axis=0, tiled=True)


def split(x):
    high = x.astype(jnp.bfloat16)
    return high, (x - high.astype(jnp.float32)).astype(jnp.bfloat16)


def dot(a, b):
    return jnp.dot(a, b, preferred_element_type=jnp.float32)


def phases(points_ref, cells_ref, stride=1):
    points = points_ref[...].astype(jnp.float32)
    count = points.shape[1]
    if stride > 1:
        old = lax.broadcasted_iota(jnp.int32, (count, count), 0)
        new = lax.broadcasted_iota(jnp.int32, (count, count), 1)
        at = old % stride * (count // stride) + old // stride
        points = jnp.dot(
            points, jnp.where(at == new, 1.0, 0.0), precision=lax.Precision.HIGHEST
        )
    exact = lax.dot_general(
        points,
        cells_ref[...].astype(jnp.float32),
        (((0,), (0,)), ((), ())),
        precision=lax.Precision.HIGHEST,
        preferred_element_type=jnp.float32,
    )
    turns = exact.astype(jnp.int32) & (KG - 1)
    angle = turns.astype(jnp.float32) * (2.0 * 3.141592653589793 / KG)
    high, low = split(jnp.concatenate([jnp.cos(angle), jnp.sin(angle)], axis=0))
    return jnp.concatenate([high, high, low], axis=1)


def turn(table, block, count):
    high, low = split(block)
    both = dot(table, jnp.concatenate([high, low, high], axis=0))
    parts = []
    for at in range(0, block.shape[1], LANES):
        cos_part = both[:count, at : at + LANES]
        sin_part = pltpu.roll(both[count:, at : at + LANES], HALF, 1)
        lane = lax.broadcasted_iota(jnp.int32, sin_part.shape, 1)
        parts.append(cos_part + jnp.where(lane < HALF, -sin_part, sin_part))
    return parts


def lay_out(x_ref, *refs, kk):
    o_ref, e_ref, p_ref, buf, held, sems, small_sems = refs[4:11]
    _, nr, modes, _, pairs = x_ref.shape
    small = [
        pltpu.make_async_copy(refs[i], refs[11 + i], small_sems.at[i]) for i in range(4)
    ]
    copies = [
        pltpu.make_async_copy(x_ref.at[:, r], buf.at[r], sems.at[r]) for r in range(nr)
    ]
    for copy in copies[:1] + small + copies[1:]:
        copy.start()
    held[...] = jnp.zeros_like(held)
    for r in range(nr):
        copies[r].wait()
        if r == nr // 2:
            for copy in small:
                copy.wait()
            e_ref[...] = phases(refs[11], refs[12], kk)
            p_ref[...] = phases(refs[13], refs[14])
        slot = r % 2
        held[slot, :modes] = buf[r, 0, :, 0, :]
        held[slot, HALF : HALF + modes] = buf[r, 1, :, 0, :]
        o_ref[pl.ds(r, pairs, stride=nr), :] = held[slot].T


def electron(t_ref, x_ref, o_ref):
    src, points = x_ref.shape[:2]
    nk = t_ref.shape[0] // 2
    table = t_ref[...]
    group = 8
    for start in range(0, points, group):
        cols = []
        for p in range(start, start + group):
            cols.append(jnp.concatenate([x_ref[i, p] for i in range(src)], axis=0))
        parts = turn(table, jnp.concatenate(cols, axis=1), nk)
        for t in range(group):
            o_ref[pl.ds(start + t, nk, stride=points), :] = parts[t]


def phonon(t_ref, x_ref, o_ref):
    nq, ns = t_ref.shape[0] // 2, t_ref.shape[1] // 3
    rows = x_ref.shape[0] // ns
    table = t_ref[...]
    group = 8
    for start in range(0, rows, group):
        cols = [x_ref[pl.ds(start + t, ns, stride=rows), :] for t in range(group)]
        parts = turn(table, jnp.concatenate(cols, axis=1), nq)
        for t in range(group):
            o_ref[pl.ds(start + t, nq, stride=rows), :] = parts[t]


def modes_of(x_ref, w_ref, o_ref, *, nk, pts, kk):
    owners = nk // kk
    w_high, w_low = split(w_ref[...])
    group = 9
    for start in range(0, pts, group):
        rows = []
        for p in range(start, start + group):
            both = [x_ref[pl.ds(m * pts + p, nk, stride=2 * pts), :] for m in range(2)]
            rows.append(jnp.concatenate(both, axis=1))
        high, low = split(jnp.concatenate(rows, axis=0))
        res = dot(high, w_high) + (dot(high, w_low) + dot(low, w_high))
        for t in range(group):
            for k in range(kk):
                at = t * nk + k * owners
                for m in range(2):
                    base = m * pts * kk + (start + t) * kk + k
                    o_ref[pl.ds(base, owners, stride=2 * pts * kk), :] = res[
                        at : at + owners, m * LANES : (m + 1) * LANES
                    ]


def finish(x_ref, o_ref, *, kk):
    modes, _, _, _, pairs = o_ref.shape
    for k in range(kk):
        turned = x_ref[pl.ds(k, pairs, stride=kk), :].T
        o_ref[:, 0, k, 0, :] = turned[:modes]
        o_ref[:, 0, k, 1, :] = turned[HALF : HALF + modes]


FAR = pl.BlockSpec(memory_space=pltpu.HBM)
WHOLE = pl.BlockSpec(memory_space=pltpu.VMEM)
ROOM = pltpu.CompilerParams(vmem_limit_bytes=20 * 2**20)


def far(x):
    return pltpu.with_memory_space_constraint(x, pltpu.HBM)


def near(x):
    return pltpu.with_memory_space_constraint(x, pltpu.VMEM)


def call(body, rows, *args):
    return pl.pallas_call(
        body,
        out_shape=pltpu.VMEM((rows, LANES), jnp.float32),
        in_specs=[WHOLE] * len(args),
        out_specs=WHOLE,
        compiler_params=ROOM,
    )(*args)


def shards(
    coupling, electron_cells, phonon_cells, kpoint_index, qpoint_index, eigenvectors, frequencies
):
    re_size = lax.axis_size("re")
    rp_size = lax.axis_size("rp")
    _, nr, _, modes, pairs = coupling.shape
    nk = kpoint_index.shape[0]
    nq = qpoint_index.shape[0]
    ns = phonon_cells.shape[0]
    peers = re_size * 2
    pts = pairs // peers
    kk = nk // re_size

    tables = [x.T for x in (kpoint_index, electron_cells, qpoint_index, phonon_cells)]
    laid, table_e, table_p = pl.pallas_call(
        functools.partial(lay_out, kk=kk),
        out_shape=[
            pltpu.VMEM((pairs * nr, LANES), jnp.float32),
            pltpu.VMEM((2 * nk, 3 * re_size * nr), jnp.bfloat16),
            pltpu.VMEM((2 * nq, 3 * ns), jnp.bfloat16),
        ],
        in_specs=[FAR] * 5,
        out_specs=[WHOLE] * 3,
        compiler_params=ROOM,
        scratch_shapes=[
            pltpu.VMEM((nr, 2, modes, 1, pairs), jnp.float32),
            pltpu.VMEM((2, LANES, pairs), jnp.float32),
            pltpu.SemaphoreType.DMA((nr,)),
            pltpu.SemaphoreType.DMA((4,)),
        ]
        + [pltpu.VMEM(x.shape, x.dtype) for x in tables],
    )(far(coupling.transpose(0, 1, 3, 2, 4)), *[far(x) for x in tables])
    got = exchange(laid.reshape(re_size, 2 * pts * nr, LANES), "re")
    got, eigenvectors, frequencies = lax.optimization_barrier((got, eigenvectors, frequencies))
    bloch_k = call(
        electron,
        nk * pts * 2,
        table_e,
        near(got.reshape(re_size, 2 * pts, nr, LANES)),
    )

    packed = jnp.concatenate(
        [eigenvectors[0].reshape(2 * modes, -1), jnp.pad(frequencies, ((0, 0), (0, modes)))]
    )
    other = lax.ppermute(packed, "mode", [(0, 1), (1, 0)])
    both = jnp.stack([packed, other])
    both = jnp.where(lax.axis_index("mode") == 0, both, both[::-1])
    scale = lax.rsqrt(2.0 * both[:, -1, :modes]).reshape(-1)
    vec = both[:, :-1].reshape(2, 2, modes, 2 * modes) * scale
    real = jnp.stack([vec[:, 0], -vec[:, 1]], axis=1)
    imag = jnp.stack([vec[:, 1], vec[:, 0]], axis=1)
    weight = jnp.stack([real, imag], axis=3)
    weight = weight.reshape(2, 2, modes, 2, 2, modes).transpose(0, 1, 2, 4, 3, 5)
    gap = HALF - modes
    weight = jnp.pad(weight, ((0, 0), (0, 0), (0, gap), (0, 0), (0, 0), (0, gap)))
    weight = weight.reshape(2 * LANES, 2 * LANES)

    got = exchange(bloch_k.reshape(rp_size, pts * 2, LANES), "rp")
    bloch_kq = call(
        phonon,
        nq * pts * 2,
        table_p,
        near(got.reshape(ns * pts * 2, LANES)),
    )

    got = exchange(bloch_kq.reshape(rp_size * 2, pts // 4, 4, LANES), ("rp", "mode"))
    rotated = call(
        functools.partial(modes_of, nk=nk, pts=pts, kk=kk),
        peers * pts * kk,
        near(got.reshape(nk * pts * 2, LANES)),
        weight,
    )

    got = exchange(rotated.reshape(peers, pts * kk, LANES), ("re", "mode"))
    return pl.pallas_call(
        functools.partial(finish, kk=kk),
        out_shape=jax.ShapeDtypeStruct((modes, 1, kk, 2, pairs), jnp.float32),
        in_specs=[WHOLE],
        out_specs=WHOLE,
        compiler_params=ROOM,
    )(near(got.reshape(pairs * kk, LANES)))


def solution(mesh):
    placed = (
        P(None, "re", "rp", "mode", None),
        P(),
        P(),
        P(),
        P(),
        P("rp", None, "mode", None),
        P("rp", "mode"),
    )
    return jax.shard_map(
        shards,
        mesh=mesh,
        in_specs=placed,
        out_specs=P("mode", "rp", "re", None, None),
        check_vma=False,
    )
```

```python
import functools

import jax
import jax.numpy as jnp
from jax import lax
from jax.experimental import pallas as pl
from jax.experimental.pallas import tpu as pltpu
from jax.sharding import PartitionSpec as P


KG = 16
LANES = 128
HALF = 64


def exchange(parts, axis):
    return lax.all_to_all(parts, axis, split_axis=0, concat_axis=0, tiled=True)


def split(x):
    high = x.astype(jnp.bfloat16)
    return high, (x - high.astype(jnp.float32)).astype(jnp.bfloat16)


def dot(a, b):
    return jnp.dot(a, b, preferred_element_type=jnp.float32)


def phases(points_ref, cells_ref, stride=1):
    points = points_ref[...].astype(jnp.float32)
    count = points.shape[1]
    if stride > 1:
        old = lax.broadcasted_iota(jnp.int32, (count, count), 0)
        new = lax.broadcasted_iota(jnp.int32, (count, count), 1)
        at = old % stride * (count // stride) + old // stride
        points = jnp.dot(
            points, jnp.where(at == new, 1.0, 0.0), precision=lax.Precision.HIGHEST
        )
    exact = lax.dot_general(
        points,
        cells_ref[...].astype(jnp.float32),
        (((0,), (0,)), ((), ())),
        precision=lax.Precision.HIGHEST,
        preferred_element_type=jnp.float32,
    )
    turns = exact.astype(jnp.int32) & (KG - 1)
    angle = turns.astype(jnp.float32) * (2.0 * 3.141592653589793 / KG)
    high, low = split(jnp.concatenate([jnp.cos(angle), jnp.sin(angle)], axis=0))
    return jnp.concatenate([high, high, low], axis=1)


def turn(table, block, count):
    high, low = split(block)
    both = dot(table, jnp.concatenate([high, low, high], axis=0))
    parts = []
    for at in range(0, block.shape[1], LANES):
        cos_part = both[:count, at : at + LANES]
        sin_part = pltpu.roll(both[count:, at : at + LANES], HALF, 1)
        lane = lax.broadcasted_iota(jnp.int32, sin_part.shape, 1)
        parts.append(cos_part + jnp.where(lane < HALF, -sin_part, sin_part))
    return parts


def lay_out(x_ref, *refs, kk):
    o_ref, e_ref, p_ref, buf, held, sems, small_sems = refs[4:11]
    _, nr, modes, _, pairs = x_ref.shape
    small = [
        pltpu.make_async_copy(refs[i], refs[11 + i], small_sems.at[i]) for i in range(4)
    ]
    copies = [
        pltpu.make_async_copy(x_ref.at[:, r], buf.at[r], sems.at[r]) for r in range(nr)
    ]
    for copy in copies[:1] + small + copies[1:]:
        copy.start()
    held[...] = jnp.zeros_like(held)
    for r in range(nr):
        copies[r].wait()
        if r == nr // 2:
            for copy in small:
                copy.wait()
            e_ref[...] = phases(refs[11], refs[12], kk)
            p_ref[...] = phases(refs[13], refs[14])
        slot = r % 2
        held[slot, :modes] = buf[r, 0, :, 0, :]
        held[slot, HALF : HALF + modes] = buf[r, 1, :, 0, :]
        o_ref[pl.ds(r, pairs, stride=nr), :] = held[slot].T


def electron(t_ref, x_ref, o_ref):
    src, points = x_ref.shape[:2]
    nk = t_ref.shape[0] // 2
    table = t_ref[...]
    group = 8
    for start in range(0, points, group):
        cols = []
        for p in range(start, start + group):
            cols.append(jnp.concatenate([x_ref[i, p] for i in range(src)], axis=0))
        parts = turn(table, jnp.concatenate(cols, axis=1), nk)
        for t in range(group):
            o_ref[pl.ds(start + t, nk, stride=points), :] = parts[t]


def phonon(t_ref, x_ref, o_ref):
    nq, ns = t_ref.shape[0] // 2, t_ref.shape[1] // 3
    rows = x_ref.shape[0] // ns
    table = t_ref[...]
    group = 8
    for start in range(0, rows, group):
        cols = [x_ref[pl.ds(start + t, ns, stride=rows), :] for t in range(group)]
        parts = turn(table, jnp.concatenate(cols, axis=1), nq)
        for t in range(group):
            o_ref[pl.ds(start + t, nq, stride=rows), :] = parts[t]


def modes_of(x_ref, w_ref, o_ref, *, nk, pts, kk):
    owners = nk // kk
    w_high, w_low = split(w_ref[...])
    group = 9
    for start in range(0, pts, group):
        rows = []
        for p in range(start, start + group):
            both = [x_ref[pl.ds(m * pts + p, nk, stride=2 * pts), :] for m in range(2)]
            rows.append(jnp.concatenate(both, axis=1))
        high, low = split(jnp.concatenate(rows, axis=0))
        res = dot(high, w_high) + (dot(high, w_low) + dot(low, w_high))
        for t in range(group):
            for k in range(kk):
                at = t * nk + k * owners
                for m in range(2):
                    base = m * owners * pts * kk + (start + t) * kk + k
                    o_ref[pl.ds(base, owners, stride=pts * kk), :] = res[
                        at : at + owners, m * LANES : (m + 1) * LANES
                    ]


def finish(x_ref, o_ref, *, kk, pts):
    modes = o_ref.shape[0]
    owners = x_ref.shape[0] // (2 * kk * pts)
    for k in range(kk):
        rows = []
        for i in range(owners):
            for m in range(2):
                at = (m * owners + i) * pts * kk + k
                rows.append(x_ref[pl.ds(at, pts, stride=kk), :])
        turned = jnp.concatenate(rows, axis=0).T
        o_ref[:, 0, k, 0, :] = turned[:modes]
        o_ref[:, 0, k, 1, :] = turned[HALF : HALF + modes]


FAR = pl.BlockSpec(memory_space=pltpu.HBM)
WHOLE = pl.BlockSpec(memory_space=pltpu.VMEM)
ROOM = pltpu.CompilerParams(vmem_limit_bytes=20 * 2**20)


def far(x):
    return pltpu.with_memory_space_constraint(x, pltpu.HBM)


def near(x):
    return pltpu.with_memory_space_constraint(x, pltpu.VMEM)


def call(body, rows, *args):
    return pl.pallas_call(
        body,
        out_shape=pltpu.VMEM((rows, LANES), jnp.float32),
        in_specs=[WHOLE] * len(args),
        out_specs=WHOLE,
        compiler_params=ROOM,
    )(*args)


def shards(
    coupling, electron_cells, phonon_cells, kpoint_index, qpoint_index, eigenvectors, frequencies
):
    re_size = lax.axis_size("re")
    rp_size = lax.axis_size("rp")
    _, nr, _, modes, pairs = coupling.shape
    nk = kpoint_index.shape[0]
    nq = qpoint_index.shape[0]
    ns = phonon_cells.shape[0]
    peers = re_size * 2
    pts = pairs // peers
    kk = nk // re_size

    tables = [x.T for x in (kpoint_index, electron_cells, qpoint_index, phonon_cells)]
    laid, table_e, table_p = pl.pallas_call(
        functools.partial(lay_out, kk=kk),
        out_shape=[
            pltpu.VMEM((pairs * nr, LANES), jnp.float32),
            pltpu.VMEM((2 * nk, 3 * re_size * nr), jnp.bfloat16),
            pltpu.VMEM((2 * nq, 3 * ns), jnp.bfloat16),
        ],
        in_specs=[FAR] * 5,
        out_specs=[WHOLE] * 3,
        compiler_params=ROOM,
        scratch_shapes=[
            pltpu.VMEM((nr, 2, modes, 1, pairs), jnp.float32),
            pltpu.VMEM((2, LANES, pairs), jnp.float32),
            pltpu.SemaphoreType.DMA((nr,)),
            pltpu.SemaphoreType.DMA((4,)),
        ]
        + [pltpu.VMEM(x.shape, x.dtype) for x in tables],
    )(far(coupling.transpose(0, 1, 3, 2, 4)), *[far(x) for x in tables])
    got = exchange(laid.reshape(re_size, 2 * pts * nr, LANES), "re")
    bloch_k = call(
        electron,
        nk * pts * 2,
        table_e,
        near(got.reshape(re_size, 2 * pts, nr, LANES)),
    )

    got = exchange(bloch_k.reshape(rp_size, pts * 2, LANES), "rp")
    bloch_kq = call(
        phonon,
        nq * pts * 2,
        table_p,
        near(got.reshape(ns * pts * 2, LANES)),
    )

    bloch_kq, eigenvectors, frequencies = lax.optimization_barrier(
        (bloch_kq, eigenvectors, frequencies)
    )
    packed = jnp.concatenate(
        [eigenvectors[0].reshape(2 * modes, -1), jnp.pad(frequencies, ((0, 0), (0, modes)))]
    )
    other = lax.ppermute(packed, "mode", [(0, 1), (1, 0)])
    both = jnp.stack([packed, other])
    both = jnp.where(lax.axis_index("mode") == 0, both, both[::-1])
    scale = lax.rsqrt(2.0 * both[:, -1, :modes]).reshape(-1)
    vec = both[:, :-1].reshape(2, 2, modes, 2 * modes) * scale
    real = jnp.stack([vec[:, 0], -vec[:, 1]], axis=1)
    imag = jnp.stack([vec[:, 1], vec[:, 0]], axis=1)
    weight = jnp.stack([real, imag], axis=3)
    weight = weight.reshape(2, 2, modes, 2, 2, modes).transpose(0, 1, 2, 4, 3, 5)
    gap = HALF - modes
    weight = jnp.pad(weight, ((0, 0), (0, 0), (0, gap), (0, 0), (0, 0), (0, gap)))
    weight = weight.reshape(2 * LANES, 2 * LANES)

    got = exchange(bloch_kq.reshape(rp_size * 2, pts // 4, 4, LANES), ("rp", "mode"))
    rotated = call(
        functools.partial(modes_of, nk=nk, pts=pts, kk=kk),
        peers * pts * kk,
        near(got.reshape(nk * pts * 2, LANES)),
        weight,
    )

    got = exchange(rotated.reshape(peers, pts * kk, LANES), ("mode", "re"))
    return pl.pallas_call(
        functools.partial(finish, kk=kk, pts=pts),
        out_shape=jax.ShapeDtypeStruct((modes, 1, kk, 2, pairs), jnp.float32),
        in_specs=[WHOLE],
        out_specs=WHOLE,
        compiler_params=ROOM,
    )(near(got.reshape(pairs * kk, LANES)))


def solution(mesh):
    placed = (
        P(None, "re", "rp", "mode", None),
        P(),
        P(),
        P(),
        P(),
        P("rp", None, "mode", None),
        P("rp", "mode"),
    )
    return jax.shard_map(
        shards,
        mesh=mesh,
        in_specs=placed,
        out_specs=P("mode", "rp", "re", None, None),
        check_vma=False,
    )
```

```python
import functools

import jax
import jax.numpy as jnp
from jax import lax
from jax.experimental import pallas as pl
from jax.experimental.pallas import tpu as pltpu
from jax.sharding import PartitionSpec as P


KG = 16
LANES = 128
HALF = 64


def exchange(parts, axis):
    return lax.all_to_all(parts, axis, split_axis=0, concat_axis=0, tiled=True)


def split(x):
    high = x.astype(jnp.bfloat16)
    return high, (x - high.astype(jnp.float32)).astype(jnp.bfloat16)


def dot(a, b):
    return jnp.dot(a, b, preferred_element_type=jnp.float32)


def phases(points_ref, cells_ref, stride=1):
    points = points_ref[...].astype(jnp.float32)
    count = points.shape[1]
    if stride > 1:
        old = lax.broadcasted_iota(jnp.int32, (count, count), 0)
        new = lax.broadcasted_iota(jnp.int32, (count, count), 1)
        at = old % stride * (count // stride) + old // stride
        points = jnp.dot(
            points, jnp.where(at == new, 1.0, 0.0), precision=lax.Precision.HIGHEST
        )
    exact = lax.dot_general(
        points,
        cells_ref[...].astype(jnp.float32),
        (((0,), (0,)), ((), ())),
        precision=lax.Precision.HIGHEST,
        preferred_element_type=jnp.float32,
    )
    turns = exact.astype(jnp.int32) & (KG - 1)
    angle = turns.astype(jnp.float32) * (2.0 * 3.141592653589793 / KG)
    high, low = split(jnp.concatenate([jnp.cos(angle), jnp.sin(angle)], axis=0))
    return jnp.concatenate([high, high, low], axis=1)


def turn(table, block, count):
    high, low = split(block)
    both = dot(table, jnp.concatenate([high, low, high], axis=0))
    parts = []
    for at in range(0, block.shape[1], LANES):
        cos_part = both[:count, at : at + LANES]
        sin_part = pltpu.roll(both[count:, at : at + LANES], HALF, 1)
        lane = lax.broadcasted_iota(jnp.int32, sin_part.shape, 1)
        parts.append(cos_part + jnp.where(lane < HALF, -sin_part, sin_part))
    return parts


def lay_out(x_ref, *refs, kk):
    o_ref, e_ref, p_ref, buf, held, sems, small_sems = refs[4:11]
    _, nr, modes, _, pairs = x_ref.shape
    small = [
        pltpu.make_async_copy(refs[i], refs[11 + i], small_sems.at[i]) for i in range(4)
    ]
    copies = [
        pltpu.make_async_copy(x_ref.at[:, r], buf.at[r], sems.at[r]) for r in range(nr)
    ]
    for copy in copies[:1] + small + copies[1:]:
        copy.start()
    held[...] = jnp.zeros_like(held)
    for r in range(nr):
        copies[r].wait()
        if r == nr // 2:
            for copy in small:
                copy.wait()
            e_ref[...] = phases(refs[11], refs[12], kk)
            p_ref[...] = phases(refs[13], refs[14])
        slot = r % 2
        held[slot, :modes] = buf[r, 0, :, 0, :]
        held[slot, HALF : HALF + modes] = buf[r, 1, :, 0, :]
        o_ref[pl.ds(r, pairs, stride=nr), :] = held[slot].T


def electron(t_ref, x_ref, o_ref):
    src, points = x_ref.shape[:2]
    nk = t_ref.shape[0] // 2
    table = t_ref[...]
    group = 8
    for start in range(0, points, group):
        cols = []
        for p in range(start, start + group):
            cols.append(jnp.concatenate([x_ref[i, p] for i in range(src)], axis=0))
        parts = turn(table, jnp.concatenate(cols, axis=1), nk)
        for t in range(group):
            o_ref[pl.ds(start + t, nk, stride=points), :] = parts[t]


def phonon(t_ref, x_ref, o_ref):
    nq, ns = t_ref.shape[0] // 2, t_ref.shape[1] // 3
    rows = x_ref.shape[0] // ns
    table = t_ref[...]
    group = 8
    for start in range(0, rows, group):
        cols = [x_ref[pl.ds(start + t, ns, stride=rows), :] for t in range(group)]
        parts = turn(table, jnp.concatenate(cols, axis=1), nq)
        for t in range(group):
            half, p = divmod(start + t, rows // 2)
            o_ref[pl.ds(half * nq * (rows // 2) + p, nq, stride=rows // 2), :] = parts[t]


def modes_of(x_ref, w_ref, o_ref, *, nk, pts, kk):
    owners = nk // kk
    w_high, w_low = split(w_ref[...])
    group = 9
    for start in range(0, pts, group):
        rows = []
        for p in range(start, start + group):
            both = [x_ref[pl.ds(m * nk * pts + p, nk, stride=pts), :] for m in range(2)]
            rows.append(jnp.concatenate(both, axis=1))
        high, low = split(jnp.concatenate(rows, axis=0))
        res = dot(high, w_high) + (dot(high, w_low) + dot(low, w_high))
        for t in range(group):
            for k in range(kk):
                at = t * nk + k * owners
                for m in range(2):
                    base = m * owners * pts * kk + (start + t) * kk + k
                    o_ref[pl.ds(base, owners, stride=pts * kk), :] = res[
                        at : at + owners, m * LANES : (m + 1) * LANES
                    ]


def finish(x_ref, o_ref, *, kk, pts):
    modes = o_ref.shape[0]
    owners = x_ref.shape[0] // (2 * kk * pts)
    for k in range(kk):
        rows = []
        for i in range(owners):
            for m in range(2):
                at = (m * owners + i) * pts * kk + k
                rows.append(x_ref[pl.ds(at, pts, stride=kk), :])
        turned = jnp.concatenate(rows, axis=0).T
        o_ref[:, 0, k, 0, :] = turned[:modes]
        o_ref[:, 0, k, 1, :] = turned[HALF : HALF + modes]


FAR = pl.BlockSpec(memory_space=pltpu.HBM)
WHOLE = pl.BlockSpec(memory_space=pltpu.VMEM)
ROOM = pltpu.CompilerParams(vmem_limit_bytes=20 * 2**20)


def far(x):
    return pltpu.with_memory_space_constraint(x, pltpu.HBM)


def near(x):
    return pltpu.with_memory_space_constraint(x, pltpu.VMEM)


def call(body, rows, *args):
    return pl.pallas_call(
        body,
        out_shape=pltpu.VMEM((rows, LANES), jnp.float32),
        in_specs=[WHOLE] * len(args),
        out_specs=WHOLE,
        compiler_params=ROOM,
    )(*args)


def shards(
    coupling, electron_cells, phonon_cells, kpoint_index, qpoint_index, eigenvectors, frequencies
):
    re_size = lax.axis_size("re")
    rp_size = lax.axis_size("rp")
    _, nr, _, modes, pairs = coupling.shape
    nk = kpoint_index.shape[0]
    nq = qpoint_index.shape[0]
    ns = phonon_cells.shape[0]
    peers = re_size * 2
    pts = pairs // peers
    kk = nk // re_size

    tables = [x.T for x in (kpoint_index, electron_cells, qpoint_index, phonon_cells)]
    laid, table_e, table_p = pl.pallas_call(
        functools.partial(lay_out, kk=kk),
        out_shape=[
            pltpu.VMEM((pairs * nr, LANES), jnp.float32),
            pltpu.VMEM((2 * nk, 3 * re_size * nr), jnp.bfloat16),
            pltpu.VMEM((2 * nq, 3 * ns), jnp.bfloat16),
        ],
        in_specs=[FAR] * 5,
        out_specs=[WHOLE] * 3,
        compiler_params=ROOM,
        scratch_shapes=[
            pltpu.VMEM((nr, 2, modes, 1, pairs), jnp.float32),
            pltpu.VMEM((2, LANES, pairs), jnp.float32),
            pltpu.SemaphoreType.DMA((nr,)),
            pltpu.SemaphoreType.DMA((4,)),
        ]
        + [pltpu.VMEM(x.shape, x.dtype) for x in tables],
    )(far(coupling.transpose(0, 1, 3, 2, 4)), *[far(x) for x in tables])
    got = exchange(laid.reshape(re_size, 2 * pts * nr, LANES), "re")
    bloch_k = call(
        electron,
        nk * pts * 2,
        table_e,
        near(got.reshape(re_size, 2 * pts, nr, LANES)),
    )

    got = exchange(bloch_k.reshape(rp_size, pts * 2, LANES), "rp")
    bloch_kq = call(
        phonon,
        nq * pts * 2,
        table_p,
        near(got.reshape(ns * pts * 2, LANES)),
    )

    bloch_kq, eigenvectors, frequencies = lax.optimization_barrier(
        (bloch_kq, eigenvectors, frequencies)
    )
    packed = jnp.concatenate(
        [eigenvectors[0].reshape(2 * modes, -1), jnp.pad(frequencies, ((0, 0), (0, modes)))]
    )
    other = lax.ppermute(packed, "mode", [(0, 1), (1, 0)])
    both = jnp.stack([packed, other])
    both = jnp.where(lax.axis_index("mode") == 0, both, both[::-1])
    scale = lax.rsqrt(2.0 * both[:, -1, :modes]).reshape(-1)
    vec = both[:, :-1].reshape(2, 2, modes, 2 * modes) * scale
    real = jnp.stack([vec[:, 0], -vec[:, 1]], axis=1)
    imag = jnp.stack([vec[:, 1], vec[:, 0]], axis=1)
    weight = jnp.stack([real, imag], axis=3)
    weight = weight.reshape(2, 2, modes, 2, 2, modes).transpose(0, 1, 2, 4, 3, 5)
    gap = HALF - modes
    weight = jnp.pad(weight, ((0, 0), (0, 0), (0, gap), (0, 0), (0, 0), (0, gap)))
    weight = weight.reshape(2 * LANES, 2 * LANES)

    got = exchange(bloch_kq.reshape(rp_size * 2, pts // 4, 4, LANES), ("mode", "rp"))
    rotated = call(
        functools.partial(modes_of, nk=nk, pts=pts, kk=kk),
        peers * pts * kk,
        near(got.reshape(nk * pts * 2, LANES)),
        weight,
    )

    got = exchange(rotated.reshape(peers, pts * kk, LANES), ("mode", "re"))
    return pl.pallas_call(
        functools.partial(finish, kk=kk, pts=pts),
        out_shape=jax.ShapeDtypeStruct((modes, 1, kk, 2, pairs), jnp.float32),
        in_specs=[WHOLE],
        out_specs=WHOLE,
        compiler_params=ROOM,
    )(near(got.reshape(pairs * kk, LANES)))


def solution(mesh):
    placed = (
        P(None, "re", "rp", "mode", None),
        P(),
        P(),
        P(),
        P(),
        P("rp", None, "mode", None),
        P("rp", "mode"),
    )
    return jax.shard_map(
        shards,
        mesh=mesh,
        in_specs=placed,
        out_specs=P("mode", "rp", "re", None, None),
        check_vma=False,
    )
```
